32 devices in a mesh: groups: 2 (over y), ep: 16 (over z, x, core), node: 1.
Axes of the slice: x: 2, y: 2, z: 4, core: 2. Of those that a mesh axis runs over, the one named last changes fastest.
Arguments:
- queries: bfloat16 [4096, 64, 576], P(('groups', 'ep'), 'node'), parts along dimension 0, may hold values from -16 to 16
- latent_kv: bfloat16 [4096, 576], P(('groups', 'ep')), parts along dimension 0, may hold values from -4 to 4
- w_value: bfloat16 [64, 512, 128], P('node'), may hold values from -0.25 to 0.25
- moe_tokens: bfloat16 [1024, 4096], P(('groups', 'ep')), parts along dimension 0, may hold values from -6 to 6
- routes: int32 [1024, 8], P(('groups', 'ep')), parts along dimension 0, may hold values from 0 to 15, all different within a row; in each aligned block of 32 rows (0 to 31, 32 to 63, ...) at most 24 rows name the same one
- router: bfloat16 [4096, 16], replicated, may hold values from -0.25 to 0.25
- w_gate: bfloat16 [16, 4096, 2048], P('ep', None, 'node'), may hold values from -0.09375 to 0.09375
- w_up: bfloat16 [16, 4096, 2048], P('ep', None, 'node'), may hold values from -0.09375 to 0.09375
- w_down: bfloat16 [16, 2048, 4096], P('ep', 'node'), may hold values from -0.125 to 0.125
Outputs:
- attention_out: bfloat16 [4096, 8192], P(('groups', 'ep'), 'node'), parts along dimension 0
- moe_out: bfloat16 [1024, 4096], P(('groups', 'ep'), 'node'), parts along dimension 0
The draws below stay inside these ranges and needn't reach their ends.
There are 2 independent parts, one for each index of `groups`. The reference program is written for one: setup_inputs(seed, part) draws one part's arguments, and reference() takes and returns one part's arrays. A program takes and returns all parts, laid end to end along the dimension named above; an argument that names none is the same for every part. Nothing has to cross between parts.
Inputs may be any that keep to these rules, and one draw needn't show every extreme that they name: `routes`: each row names 8 different experts; among the 32 rows of one index of ep no expert is named by more than 24 rows, a bound that some block reaches of them.
All inputs are finite; a program needn't handle non-finite values.
Results may differ from the reference program's by a relative error of at most 0.015.
Values may be sent and summed in bfloat16 or wider, within the bound.
A program may use at most 192 MiB of HBM per device.

```python
import math
import jax
import jax.numpy as jnp
import numpy as np
from jax import lax

D = 4096
FF = 2048
HEADS = 64
LATENT = 512
ROPE = 64
VHEAD = 128
TOPK = 8
EXPERTS = 16
SEQ_DEV = 128
SEQ = 2048
TB_DEV = 32
TOKB = 512
CAP = 24
N_EP = 16
N_NODE = 1


def attention_pair(key):
    width = LATENT + ROPE
    latent_key, query_key = jax.random.split(jax.random.fold_in(key, 11), 2)
    latent = jnp.clip(jax.random.normal(latent_key, (SEQ, width), jnp.float32), -4.0, 4.0)
    queries = jnp.clip(jax.random.normal(query_key, (SEQ, HEADS, width), jnp.float32), -4.0, 4.0)
    return (latent, queries)


def draw_queries(key, part):
    return attention_pair(key)[1].astype(jnp.bfloat16)


def draw_latent_kv(key, part):
    return attention_pair(key)[0].astype(jnp.bfloat16)


def shard_levels(stream_key, dims, shards, low, largest):
    loudness = 1.0
    for dim, shards_of in shards:
        draws = jax.random.uniform(jax.random.fold_in(jax.random.fold_in(stream_key, 6), dim), (shards_of,), jnp.float32, low / len(shards), largest / len(shards))
        loudness = loudness * jnp.repeat(jnp.exp(draws), dims[dim] // shards_of).reshape((-1,) + (1,) * (len(dims) - 1 - dim))
    return loudness


def shared_out(own_key, own, number, rows, count, top, limit, lean):
    ranking = jax.random.permutation(own_key, count)
    crowded, usual = portions_of(count, rows * top, limit, lean, True), portions_of(count, rows * top, limit, lean, False)
    places = jnp.arange(count)

    def named(tallies, offset_by):
        used = int((tallies > 0).sum())
        fixed = max(1, used // 4)
        moved = fixed + (places - fixed + offset_by * (used - fixed)) % max(1, count - fixed)
        return jnp.zeros((count,), jnp.int32).at[ranking[jnp.where(places < fixed, places, moved)]].set(jnp.asarray(tallies, jnp.int32))

    tallies = jnp.where(number % 4 == 0, named(crowded, number // 4), named(usual, number - number // 4 - 1))
    mixed = jax.random.permutation(jax.random.fold_in(own, 3), count)
    source_of, receiver = mixed[0:count // 2 * 2:2], mixed[1:count // 2 * 2:2]
    margin = jnp.minimum(tallies[source_of] - 1, limit - tallies[receiver]) // 2
    margin = jnp.where((source_of == ranking[0]) | (receiver == ranking[0]) | (tallies[receiver] == 0), 0, jnp.maximum(margin, 0))
    moved = jax.random.randint(jax.random.fold_in(own, 4), (count // 2,), 0, 1 << 20) % (margin + 1)
    tallies = tallies.at[source_of].add(-moved).at[receiver].add(moved)
    labels = jnp.searchsorted(jnp.cumsum(tallies), jnp.arange(rows * top), side="right").astype(jnp.int32)
    table = labels.reshape(top, rows).T
    table = table[jax.random.permutation(jax.random.fold_in(own, 1), rows)]
    offset_by = jax.random.randint(jax.random.fold_in(own, 2), (rows, 1), 0, top)
    return jnp.take_along_axis(table, (jnp.arange(top)[None, :] + offset_by) % top, axis=1)


def portions_of(count, total, reach, skew, full):
    portions = [(1 << 20) // math.isqrt(grade ** skew) + 1 for grade in range(1, count + 1)]
    largest = reach if full else min(reach, max(-(-total // count), total * portions[0] // sum(portions)))
    least = 1 if total - largest >= count - 1 else 0
    holding, rest = [largest] + [least] * (count - 1), total - largest - least * (count - 1)
    while rest > 0:
        candidates = [i for i in range(1, count) if holding[i] < largest] or [i for i in range(1, count) if holding[i] < reach]
        mass, left = sum([portions[i] for i in candidates]), rest
        for i in candidates:
            extra = min(reach - holding[i], max(1, left * portions[i] // mass), rest)
            holding[i] = holding[i] + extra
            rest = rest - extra
    return np.array(holding)


def centred(rng, extent, scale, reach, cuts=(), held_as=jnp.bfloat16):
    values = jax.random.normal(rng, extent, jnp.float32) * scale
    if len(cuts) > 0:
        values = shard_levels(rng, extent, cuts, -0.22, 0.18) * values
    return jnp.clip(values, min=-reach, max=reach).astype(held_as)


def setup_inputs(seed: int = 0, part: int = 0) -> dict:
    streams_of = jax.random.split(jax.random.key(seed), 10)
    part_keys = jax.random.split(jax.random.fold_in(streams_of[9], part), 10)
    queries = draw_queries(jax.random.fold_in(jax.random.fold_in(streams_of[9], part), 71), part)
    latent_kv = draw_latent_kv(jax.random.fold_in(jax.random.fold_in(streams_of[9], part), 71), part)
    w_value = centred(streams_of[2], (HEADS, LATENT, VHEAD), LATENT ** -0.5, 0.25)
    moe_tokens = centred(part_keys[3], (TOKB, D), 1.0, 6.0, ((0, 16),))
    routes_keys = jax.random.split(jax.random.fold_in(part_keys[4], 1), TOKB // TB_DEV)
    routes_turns = jax.random.permutation(jax.random.fold_in(part_keys[4], 3), TOKB // TB_DEV)
    routes = jax.vmap(lambda own, number: shared_out(jax.random.fold_in(part_keys[4], 2), own, number, TB_DEV, EXPERTS, TOPK, CAP, 1))(routes_keys, routes_turns).reshape((TOKB, TOPK))
    router = centred(streams_of[5], (D, EXPERTS), (D // 9) ** -0.5, 0.25)
    w_gate = centred(streams_of[6], (EXPERTS, D, FF), D ** -0.5, 0.09375, ((0, 16),))
    w_up = centred(streams_of[7], (EXPERTS, D, FF), D ** -0.5, 0.09375, ((0, 16),))
    w_down = centred(streams_of[8], (EXPERTS, FF, D), FF ** -0.5, 0.125, ((0, 16),))
    return {"queries": queries, "latent_kv": latent_kv, "w_value": w_value, "moe_tokens": moe_tokens, "routes": routes, "router": router, "w_gate": w_gate, "w_up": w_up, "w_down": w_down}


ROUTED_SCALE = 2.5


def attend_rows(block, first, latent_kv, w_value):
    width = latent_kv.shape[1]
    latent_width = w_value.shape[1]
    scale = (w_value.shape[2] + width - latent_width) ** -0.5
    scores = jnp.einsum("qhc,kc->qhk", block.astype(jnp.float32), latent_kv.astype(jnp.float32)) * scale
    query_pos = first + jnp.arange(block.shape[0], dtype=jnp.int32)
    key_pos = jnp.arange(latent_kv.shape[0], dtype=jnp.int32)
    visible = key_pos[None, None, :] <= query_pos[:, None, None]
    scores = jnp.where(visible, scores, -1.0e30)
    row_max = jnp.max(scores, axis=2, keepdims=True)
    raised = jnp.where(visible, jnp.exp(scores - row_max), 0.0)
    totals = jnp.sum(raised, axis=2, keepdims=True)
    probs = lax.optimization_barrier(raised.astype(jnp.bfloat16)).astype(jnp.float32)
    values = latent_kv[:, :latent_width].astype(jnp.float32)
    context = jnp.einsum("qhk,kc->qhc", probs, values) / totals
    context = lax.optimization_barrier(context.astype(jnp.bfloat16)).astype(jnp.float32)
    result = jnp.einsum("qhc,hcv->qhv", context, w_value.astype(jnp.float32))
    return result.astype(jnp.bfloat16).reshape(block.shape[0], -1)


def attention_part(queries, latent_kv, w_value):
    blocks = queries.reshape(N_EP, SEQ_DEV, queries.shape[1], queries.shape[2])
    firsts = jnp.arange(N_EP, dtype=jnp.int32) * SEQ_DEV

    def one_block(packed):
        return attend_rows(packed[0], packed[1], latent_kv, w_value)

    outputs = lax.map(one_block, (blocks, firsts))
    return outputs.reshape(queries.shape[0], -1)


def moe_part(moe_tokens, routes, router, w_gate, w_up, w_down):
    tokens_all, top = routes.shape
    experts = router.shape[1]
    logits = jnp.dot(moe_tokens, router, preferred_element_type=jnp.float32)
    affinity = jax.nn.sigmoid(logits)
    chosen = jnp.take_along_axis(affinity, routes, axis=1)
    gates = ROUTED_SCALE * chosen / jnp.sum(chosen, axis=1, keepdims=True)
    blocks = routes.reshape(N_EP, TB_DEV, top)
    expert_range = jnp.arange(experts, dtype=jnp.int32)
    member = jnp.any(blocks[:, :, :, None] == expert_range[None, None, None, :], axis=2).astype(jnp.int32)
    before = jnp.cumsum(member, axis=1) - member
    slots = jnp.take_along_axis(before, blocks, axis=2)
    rows = (jnp.arange(N_EP, dtype=jnp.int32)[:, None, None] * CAP + slots).reshape(-1)
    expert_ids = routes.reshape(-1)
    token_ids = jnp.repeat(jnp.arange(tokens_all, dtype=jnp.int32), top)
    table = jnp.zeros((experts, N_EP * CAP), jnp.int32).at[expert_ids, rows].set(token_ids)
    weights = jnp.zeros((experts, N_EP * CAP), jnp.float32).at[expert_ids, rows].set(gates.reshape(-1))

    def one_expert(total, packed):
        row_ids, row_gates, gate_w, up_w, down_w = packed
        inputs = moe_tokens[row_ids]
        gate = jnp.dot(inputs, gate_w, preferred_element_type=jnp.float32)
        upward = jnp.dot(inputs, up_w, preferred_element_type=jnp.float32)
        hidden = lax.optimization_barrier((jax.nn.silu(gate) * upward).astype(jnp.bfloat16)).astype(jnp.float32)
        pieces = hidden.reshape(row_ids.shape[0], N_NODE, -1)
        downs = down_w.reshape(N_NODE, -1, down_w.shape[1]).astype(jnp.float32)
        partial_value = jnp.einsum("rbf,bfd->rbd", pieces, downs)
        partial_value = lax.optimization_barrier(partial_value.astype(jnp.bfloat16)).astype(jnp.float32)
        summed = jnp.sum(partial_value, axis=1)
        return total.at[row_ids].add(row_gates[:, None] * summed), None

    start = jnp.zeros((tokens_all, moe_tokens.shape[1]), jnp.float32)
    total, ignored = lax.scan(one_expert, start, (table, weights, w_gate, w_up, w_down))
    return total.astype(jnp.bfloat16)


def reference(queries, latent_kv, w_value, moe_tokens, routes, router, w_gate, w_up, w_down):
    attention_out = attention_part(queries, latent_kv, w_value)
    moe_out = moe_part(moe_tokens, routes, router, w_gate, w_up, w_down)
    return (attention_out, moe_out)
```

```python
import functools

import jax
import jax.numpy as jnp
from jax import lax
from jax.experimental import pallas as pl
from jax.experimental.pallas import tpu as pltpu
from jax.sharding import PartitionSpec as P

ROUTED_SCALE = 2.5
NEGATIVE = -1e30
LOG2E = 1.4426950408889634


def attend_kernel(per_sub, scale, me_ref, q_ref, kv_ref, wv_ref, *rest):
    out_ref = rest[-1]
    heads, seq_dev, width = q_ref.shape
    keys = kv_ref.shape[0]
    latent_width, value_width = wv_ref.shape[1], wv_ref.shape[2]
    first = me_ref[0] * seq_dev
    rows = per_sub * seq_dev
    for sub in range(heads // per_sub):
        q = q_ref[sub * per_sub : (sub + 1) * per_sub].reshape(rows, width)
        scores = lax.dot_general(
            q, kv_ref[...], (((1,), (1,)), ((), ())), preferred_element_type=jnp.float32
        )
        row = lax.broadcasted_iota(jnp.int32, (rows, keys), 0)
        col = lax.broadcasted_iota(jnp.int32, (rows, keys), 1)
        scores = jnp.where(col <= lax.rem(row, seq_dev) + first, scores, NEGATIVE)
        row_max = jnp.max(scores, axis=1, keepdims=True)
        raised = jnp.exp2((scores - row_max) * (scale * LOG2E))
        totals = jnp.sum(raised, axis=1, keepdims=True)
        context = jnp.dot(
            raised.astype(jnp.bfloat16),
            kv_ref[:, :latent_width],
            preferred_element_type=jnp.float32,
        )
        context = (context / totals).astype(jnp.bfloat16)
        for h in range(per_sub):
            head = sub * per_sub + h
            out_ref[:, head * value_width : (head + 1) * value_width] = jnp.dot(
                context[h * seq_dev : (h + 1) * seq_dev],
                wv_ref[head],
                preferred_element_type=jnp.float32,
            ).astype(out_ref.dtype)


def attend(me, q, kv, w_value, start, count, scale, prior):
    heads, seq_dev, width = q.shape
    _, latent_width, value_width = w_value.shape
    keys = kv.shape[0]
    block = min(8, count)
    per_sub = 2 if block % 2 == 0 else 1
    offset = start // block
    in_specs = [
        pl.BlockSpec(memory_space=pltpu.SMEM),
        pl.BlockSpec((block, seq_dev, width), lambda i: (i + offset, 0, 0)),
        pl.BlockSpec((keys, width), lambda i: (0, 0)),
        pl.BlockSpec((block, latent_width, value_width), lambda i: (i + offset, 0, 0)),
    ]
    args = [me, q, kv, w_value]
    aliases = {}
    if prior is not None:
        in_specs.append(pl.BlockSpec(memory_space=pl.ANY))
        args.append(prior)
        aliases = {4: 0}
    return pl.pallas_call(
        functools.partial(attend_kernel, per_sub, scale),
        grid=(count // block,),
        in_specs=in_specs,
        out_specs=pl.BlockSpec((seq_dev, block * value_width), lambda i: (0, i + offset)),
        out_shape=jax.ShapeDtypeStruct((seq_dev, heads * value_width), jnp.bfloat16),
        input_output_aliases=aliases,
        compiler_params=pltpu.CompilerParams(vmem_limit_bytes=56 * 1024 * 1024),
        cost_estimate=pl.CostEstimate(
            flops=2 * count * seq_dev * keys * (width + latent_width),
            bytes_accessed=2 * count * (seq_dev * width + latent_width * value_width),
            transcendentals=count * seq_dev * keys,
        ),
    )(*args)


def per_device(queries, latent_kv, w_value, moe_tokens, routes, router, w_gate, w_up, w_down):
    seq_dev, heads_dev, width = queries.shape
    latent_width, value_width = w_value.shape[1], w_value.shape[2]
    scale = (value_width + width - latent_width) ** (-0.5)
    me = lax.axis_index("ep")
    me_array = jnp.full((1,), me, jnp.int32)
    tokens_dev, top = routes.shape
    local_experts = w_gate.shape[0]
    ep_size = lax.axis_size("ep")
    experts = local_experts * ep_size
    model = moe_tokens.shape[1]
    tokens = tokens_dev * ep_size
    capacity = min(tokens_dev, 3 * tokens_dev * top // (2 * experts))
    slots = capacity * ep_size

    kv = lax.all_gather(latent_kv, "ep", axis=0, tiled=True)
    q = jnp.transpose(queries, (1, 0, 2))

    logits = jnp.dot(moe_tokens, router, preferred_element_type=jnp.float32)
    affinity = jax.nn.sigmoid(logits)
    named = jnp.any(routes[:, :, None] == lax.iota(jnp.int32, experts)[None, None, :], axis=1)
    kept = jnp.where(named, affinity, 0.0)
    gates = ROUTED_SCALE * kept / jnp.sum(kept, axis=1, keepdims=True)
    gate_high = gates.astype(jnp.bfloat16)
    gate_low = (gates - gate_high.astype(jnp.float32)).astype(jnp.bfloat16)
    extra = jnp.concatenate([gate_high, gate_low, named.astype(jnp.bfloat16)], axis=1)
    extra = jnp.pad(extra, ((0, 0), (0, -extra.shape[1] % 128)))
    outgoing = jnp.concatenate([moe_tokens, extra], axis=1)
    kv, outgoing, q = lax.optimization_barrier((kv, outgoing, q))
    packed = lax.all_gather(outgoing, "ep", axis=0, tiled=True)

    half = heads_dev // 2
    attention_out = attend(me_array, q, kv, w_value, 0, half, scale, None)

    packed, attention_out = lax.optimization_barrier((packed, attention_out))
    all_tokens = packed[:, :model]
    extras = packed[:, model:].astype(jnp.float32)
    contributions = jnp.zeros((tokens, model), jnp.float32)
    lower = (lax.iota(jnp.int32, tokens)[:, None] > lax.iota(jnp.int32, tokens)[None, :])
    for j in range(local_experts):
        mine = (lax.iota(jnp.int32, experts) == me * local_experts + j).astype(jnp.float32)
        pick = lambda k: jnp.sum(extras[:, k * experts : (k + 1) * experts] * mine, axis=1)
        gate_of = pick(0) + pick(1)
        member = pick(2)
        rank = jnp.dot(
            lower.astype(jnp.bfloat16),
            member.astype(jnp.bfloat16)[:, None],
            preferred_element_type=jnp.float32,
        )[:, 0].astype(jnp.int32)
        slot = jnp.where(member > 0, rank, -1)
        chosen = (slot[None, :] == lax.iota(jnp.int32, slots)[:, None]).astype(jnp.bfloat16)
        rows = jnp.dot(chosen, all_tokens, preferred_element_type=jnp.float32).astype(jnp.bfloat16)
        gate = jnp.dot(rows, w_gate[j], preferred_element_type=jnp.float32)
        upward = jnp.dot(rows, w_up[j], preferred_element_type=jnp.float32)
        hidden = (jax.nn.silu(gate) * upward).astype(jnp.bfloat16)
        partial_value = jnp.dot(hidden, w_down[j], preferred_element_type=jnp.float32)
        spread = lax.dot_general(
            chosen,
            partial_value.astype(jnp.bfloat16),
            (((0,), (0,)), ((), ())),
            preferred_element_type=jnp.float32,
        )
        contributions = contributions + gate_of[:, None] * spread
    contributions = contributions.astype(jnp.bfloat16)
    moe_out = lax.psum_scatter(contributions, "ep", scatter_dimension=0, tiled=True)
    if lax.axis_size("node") > 1:
        moe_out = lax.psum_scatter(moe_out, "node", scatter_dimension=1, tiled=True)

    contributions, attention_out = lax.optimization_barrier((contributions, attention_out))
    attention_out = attend(
        me_array, q, kv, w_value, half, heads_dev - half, scale, attention_out
    )
    return (attention_out, moe_out)


def solution(mesh):
    placed = (
        P(("groups", "ep"), "node", None),
        P(("groups", "ep"), None),
        P("node", None, None),
        P(("groups", "ep"), None),
        P(("groups", "ep"), None),
        P(),
        P("ep", None, "node"),
        P("ep", None, "node"),
        P("ep", "node", None),
    )
    return jax.shard_map(
        per_device,
        mesh=mesh,
        in_specs=placed,
        out_specs=(P(("groups", "ep"), "node"), P(("groups", "ep"), "node")),
        check_vma=False,
    )
```
